512 devices in a mesh: replica: 64 (over y, z_lo, core), tensor: 8 (over z_hi, x).
Axes of the slice: x: 4, y: 4, z: 16 (z_hi: 2, z_lo: 8; z = z_hi * 8 + z_lo), core: 2. Of those that a mesh axis runs over, the one named last changes fastest.
Arguments:
- hidden_act: bfloat16 [16384, 7168], P('replica', 'tensor'), may hold values from -15 to 15
- residual_in: bfloat16 [512, 65536], P('tensor', 'replica'), may hold values from -6 to 6
- cotangent: bfloat16 [512, 65536], P('tensor', 'replica'), may hold values from -6 to 6
- norm_gain: bfloat16 [2048], replicated, may hold values from 0.25 to 1.75
- inner_weight: bfloat16 [7168, 65536], P('tensor', 'replica'), may hold values from -24 to 24
- anchor: bfloat16 [7168, 2048], P('tensor', 'replica'), may hold values from -6 to 6
- momentum: bfloat16 [7168, 2048], P('tensor', 'replica'), may hold values from -3 to 3
Outputs:
- normed: bfloat16 [512, 65536], P('tensor', 'replica')
- mixed_weight: bfloat16 [7168, 65536], P('tensor', 'replica')
- momentum_out: bfloat16 [7168, 2048], P('tensor', 'replica')
The draws below stay inside these ranges and needn't reach their ends.
All inputs are finite; a program needn't handle non-finite values.
Results may differ from the reference program's by a relative error of at most 0.0075.
Values may be sent and summed in bfloat16 or wider, within the bound.
A program may use at most 64 MiB of HBM per device.

```python
import math
import jax
import jax.numpy as jnp
from jax import lax

D = 2048
FF = 7168
TOK = 512
REPLICAS = 32
ROWS = 16384


def draw_hidden_act(key, part):
    key_base, key_jitter = jax.random.split(jax.random.fold_in(key, 11))
    column = jnp.arange(FF, dtype=jnp.float32) / max(FF - 1, 1)
    ramp = 0.6 + 1.2 * column
    jitter = jnp.exp(jax.random.uniform(key_jitter, (FF,), jnp.float32, -0.7, 0.7))
    base = jnp.clip(jax.random.normal(key_base, (ROWS, FF), jnp.float32), -4.0, 4.0)
    return (base * ramp * jitter).astype(jnp.bfloat16)


def draw_inner_weight(key, part):
    key_base = jax.random.fold_in(key, 23)
    base = jnp.clip(jax.random.normal(key_base, (FF, REPLICAS * D), jnp.float32), -6.0, 6.0)
    column = jnp.arange(REPLICAS * D, dtype=jnp.int32)
    owner = column // D
    within = column % D
    marked = within * REPLICAS // D == owner
    factor = jnp.where(marked, 4.0, 1.0).astype(jnp.float32)
    return (base * factor[None, :]).astype(jnp.bfloat16)


def shard_levels(key, shape, cuts, least, top_value):
    level = 1.0
    for position, shards_of in cuts:
        draws = jax.random.uniform(jax.random.fold_in(jax.random.fold_in(key, 6), position), (shards_of,), jnp.float32, least / len(cuts), top_value / len(cuts))
        level = level * jnp.repeat(jnp.exp(draws), shape[position] // shards_of).reshape((-1,) + (1,) * (len(shape) - 1 - position))
    return level


def normal_values(key, dims, scale, most, cuts=(), kind=jnp.bfloat16):
    entries = scale * jax.random.normal(key, dims, jnp.float32)
    if cuts:
        entries = entries * shard_levels(key, dims, cuts, -0.22, 0.18)
    return jnp.clip(entries, -most, most).astype(kind)


def setup_inputs(seed: int = 0) -> dict:
    arg_keys = jax.random.split(jax.random.key(seed), 8)
    hidden_act = draw_hidden_act(jax.random.fold_in(arg_keys[7], 71), 0)
    residual_in = normal_values(arg_keys[1], (TOK, REPLICAS * D), 1.0, 6.0, ((0, 8), (1, 64)))
    cotangent = normal_values(arg_keys[2], (TOK, REPLICAS * D), 1.0, 6.0, ((0, 8), (1, 64)))
    norm_gain = jnp.clip(1.0 + 0.15 * jax.random.normal(arg_keys[3], (D,), jnp.float32), 0.25, 1.75).astype(jnp.bfloat16)
    inner_weight = draw_inner_weight(jax.random.fold_in(arg_keys[7], 71), 0)
    anchor = normal_values(arg_keys[5], (FF, D), 1.0, 6.0, ((0, 8), (1, 64)))
    momentum = normal_values(arg_keys[6], (FF, D), 0.5, 3.0, ((0, 8), (1, 64)))
    return {"hidden_act": hidden_act, "residual_in": residual_in, "cotangent": cotangent, "norm_gain": norm_gain, "inner_weight": inner_weight, "anchor": anchor, "momentum": momentum}


inner_rate = 0.2
outer_rate = 0.7
outer_mu = 0.9
mix_share = 0.5

def reference(hidden_act, residual_in, cotangent, norm_gain, inner_weight, anchor, momentum):
    multiplier = 1.0 / math.sqrt(FF)
    step_scale = inner_rate * math.sqrt(FF / TOK)
    norm_scale = norm_gain.astype(jnp.float32)

    def add_weight(index, carry):
        start = (index * D).astype(jnp.int32)
        return carry + lax.dynamic_slice_in_dim(inner_weight, start, D, 1).astype(jnp.float32)
    summed = lax.fori_loop(0, REPLICAS, add_weight, jnp.zeros((FF, D), jnp.float32))
    anchor_f = anchor.astype(jnp.float32)
    pseudo = anchor_f - summed / REPLICAS
    moment = (outer_mu * momentum.astype(jnp.float32) + pseudo).astype(jnp.bfloat16)
    new_anchor = (anchor_f - outer_rate * (pseudo + outer_mu * moment.astype(jnp.float32))).astype(jnp.bfloat16)
    anchor_new_f = new_anchor.astype(jnp.float32)

    def one_replica(index, carry):
        normed_all, mixed_all = carry
        col_start = (index * D).astype(jnp.int32)
        row_start = (index * TOK).astype(jnp.int32)
        hidden_rows = lax.dynamic_slice_in_dim(hidden_act, row_start, TOK, 0)
        layer_weight = lax.dynamic_slice_in_dim(inner_weight, col_start, D, 1)
        resid_rows = lax.dynamic_slice_in_dim(residual_in, col_start, D, 1)
        cot_rows = lax.dynamic_slice_in_dim(cotangent, col_start, D, 1)
        out_rows = jnp.dot(hidden_rows, layer_weight, preferred_element_type=jnp.float32) * multiplier
        summed_in = resid_rows.astype(jnp.float32) + out_rows
        root_inv = lax.rsqrt(lax.optimization_barrier(jnp.mean(summed_in * summed_in, axis=-1, keepdims=True)) + 1e-05)
        normed = (summed_in * root_inv * norm_scale).astype(normed_all.dtype)
        dz_rows = cot_rows.astype(jnp.float32) * norm_scale
        inner_mean = lax.optimization_barrier(jnp.mean(dz_rows * summed_in, axis=-1, keepdims=True))
        slopes = (root_inv * (dz_rows - summed_in * inner_mean * root_inv * root_inv)).astype(jnp.bfloat16)
        gradient = jnp.dot(hidden_rows.T, slopes, preferred_element_type=jnp.float32) * multiplier
        stepped = layer_weight.astype(jnp.float32) - step_scale * gradient
        mixed = (mix_share * stepped + (1.0 - mix_share) * anchor_new_f).astype(mixed_all.dtype)
        zero = jnp.zeros((), jnp.int32)
        normed_all = lax.dynamic_update_slice(normed_all, normed, (zero, col_start))
        mixed_all = lax.dynamic_update_slice(mixed_all, mixed, (zero, col_start))
        return (normed_all, mixed_all)
    start_normed = jnp.zeros((TOK, REPLICAS * D), jnp.bfloat16)
    start_mixed = jnp.zeros((FF, REPLICAS * D), jnp.bfloat16)
    normed_all, mixed_all = lax.fori_loop(0, REPLICAS, one_replica, (start_normed, start_mixed))
    return (normed_all, mixed_all, moment)
```

```python
import math

import jax
import jax.numpy as jnp
from jax import lax
from jax.experimental import pallas as pl
from jax.experimental.pallas import tpu as pltpu
from jax.sharding import PartitionSpec as P

FF = 7168
TOK = 512

inner_rate = 0.2
outer_rate = 0.7
outer_mu = 0.9
mix_share = 0.5

F32 = jnp.float32
BF16 = jnp.bfloat16
ROWS = 896
COLS = 1024
CHUNKS = ((0, 512), (512, 384))
REPLICAS = 32
FEATURES = 2048
MULT = 1.0 / math.sqrt(FF)
STEP = inner_rate * math.sqrt(FF / TOK)
NSEM = 72


def kernel(
    h_hbm, r_hbm, c_hbm, gain, w_hbm, at_hbm, mt_hbm,
    normed_hbm, mixed_hbm, mout_hbm,
    wv, hb, ht, p32, pb, ap1, ap2, xown, zsend, zrecv, rv, cv, stat_out, stat_in, sb, nout,
    p1buf, cbuf, yrecv, yown, tt, q1r, qs, near, far, atv, mtv, nown, mo, ta, na, nfull,
    base, mix, send, recv, loc,
):
    ri = lax.axis_index("replica")
    ti = lax.axis_index("tensor")
    s = lax.rem(ri, 2)
    chip = lax.div(ri, 2)
    z = lax.rem(chip, 8)
    y = lax.div(chip, 8)
    zh = lax.div(ti, 4)
    x = lax.rem(ti, 4)
    q = lax.div(z, 4)
    p = lax.rem(z, 4)
    zfar = 4 * (1 - q) + p
    o = 1 - s
    sy = lax.div(y, 2)
    je = lax.rem(y, 2)
    jo = 1 - je
    yb = 2 * s + jo
    plus = lax.rem(yb - y + 4, 4) == 1
    hc = jnp.where(plus, 1, 0)
    hd = 1 - hc
    side = 1 - hc
    yo = lax.rem(2 * y - yb + 4, 4)
    yup = lax.rem(y + 1, 4)
    ydn = lax.rem(y + 3, 4)
    xup = lax.rem(x + 1, 4)
    xdn = lax.rem(x + 3, 4)
    xfar = lax.rem(x + 2, 4)
    own = s == sy
    is_near = s == q

    def dev(yy=y, zz=z, cc=s, hh=zh, xx=x):
        return ((yy * 8 + zz) * 2 + cc, hh * 4 + xx)

    ids = {}
    used = {"r": 0, "s": 0}

    def sid(name, count=1):
        if name not in ids:
            kind = "r" if name.startswith("r_") else "s"
            ids[name] = used[kind]
            used[kind] += count
            assert used[kind] <= NSEM
        return ids[name]

    pending = []

    def when(cond, f):
        if cond is None:
            f()
        else:
            pl.when(cond)(f)

    other = dev(cc=o)

    def go(sname, ridx, src, dst, device, cond=None):
        d = pltpu.make_async_remote_copy(
            src_ref=src, dst_ref=dst, send_sem=send.at[sid("s_" + sname)], recv_sem=recv.at[ridx],
            device_id=device, device_id_type=pl.DeviceIdType.MESH,
        )
        when(cond, d.start)
        pending.append((cond, d))

    def got(ridx, dst, cond=None):
        d = pltpu.make_async_remote_copy(
            src_ref=dst, dst_ref=dst, send_sem=send.at[0], recv_sem=recv.at[ridx],
            device_id=other, device_id_type=pl.DeviceIdType.MESH,
        )
        when(cond, d.wait_recv)

    nloc = [0]

    def local_copy(src, dst):
        d = pltpu.make_async_copy(src, dst, loc.at[nloc[0]])
        nloc[0] += 1
        return d

    peers = [other, dev(xx=xup), dev(xx=xdn), dev(hh=1 - zh)]
    for yy in (yup, ydn):
        peers += [dev(yy=yy, cc=0), dev(yy=yy, cc=1)]
    for k in (1, 2, 3):
        peers.append(dev(zz=4 * q + lax.rem(p + k, 4)))
    peers += [dev(zz=zfar, cc=0), dev(zz=zfar, cc=1)]
    lw = local_copy(w_hbm, wv)
    lh = local_copy(h_hbm, hb.at[s])
    lr = local_copy(r_hbm, rv)
    lc = local_copy(c_hbm, cv)
    la = local_copy(at_hbm, atv)
    lm = local_copy(mt_hbm, mtv)
    for d in (lh, lw, lr, lc, la, lm):
        d.start()
    barrier = pltpu.get_barrier_semaphore()
    for peer in peers:
        pl.semaphore_signal(barrier, inc=1, device_id=peer, device_id_type=pl.DeviceIdType.MESH)
    pl.semaphore_wait(barrier, len(peers))

    def lane(value):
        return pl.multiple_of(value, 256)

    def wcols(j, h):
        return pl.ds(lane(j * 512 + h * 256), 256)

    go("h", sid("r_h"), h_hbm, hb.at[s], other)

    own_local = []
    for k, (r0, n) in enumerate(CHUNKS):
        rows = pl.ds(r0, n)
        rp1 = sid(f"r_p1{k}")
        ryo = sid(f"r_yo{k}")
        go(f"p1a{k}", rp1, w_hbm.at[rows, wcols(je, 0)], p1buf.at[rows], dev(yy=ydn), jnp.logical_not(own))
        go(f"p1b{k}", rp1, w_hbm.at[rows, wcols(je, 1)], p1buf.at[rows], dev(yy=yup), jnp.logical_not(own))
        go(f"yo{k}", ryo, w_hbm.at[rows, wcols(je, o)], yown.at[rows], other, own)
        d = local_copy(w_hbm.at[rows, wcols(je, s)], yown.at[rows])
        when(own, d.start)
        own_local.append(d)
    for k, (r0, n) in enumerate(CHUNKS):
        rows = pl.ds(r0, n)
        ryr = sid(f"r_yr{k}", 2)
        go(f"yd{k}", ryr + side, w_hbm.at[rows, wcols(jo, hd)], yrecv.at[side, rows], dev(yy=yb, cc=hd))

    def partial_out(half):
        @pl.loop(0, COLS // 256)
        def _(i):
            cols = pl.ds(lane(i * 256), 256)
            v = jnp.dot(hb[half], wv[:, cols], preferred_element_type=F32).reshape(4, 64, 256)
            p32[half, :, :, cols] = v
            pb[half, :, :, cols] = v.astype(BF16)

    lh.wait()
    lw.wait()
    partial_out(s)
    got(sid("r_h"), hb.at[o])
    partial_out(o)

    halves = (1 - zh, zh)
    for k, hf in enumerate(halves):
        ra = sid(f"r_ap1{k}", 2)
        go(f"ap1a{k}", ra, pb.at[hf, xfar, pl.ds(0, 32)], ap1.at[k, 0], dev(xx=xdn))
        go(f"ap1b{k}", ra + 1, pb.at[hf, xfar, pl.ds(32, 32)], ap1.at[k, 1], dev(xx=xup))

    def combine(k):
        r0, n = CHUNKS[k]
        rows = pl.ds(r0, n)
        got(sid(f"r_p1{k}"), p1buf.at[rows])

        @pl.loop(0, n // 128)
        def _(i):
            t = pl.ds(pl.multiple_of(r0 + i * 128, 128), 128)
            cbuf[t, :] = (wv[t, wcols(jo, hc)].astype(F32) + p1buf[t, :].astype(F32)).astype(BF16)

        go(f"yc{k}", sid(f"r_yr{k}") + side, cbuf.at[rows], yrecv.at[side, rows], dev(yy=yb, cc=hc))

    combine(0)
    combine(1)

    for k, hf in enumerate(halves):
        ra = sid(f"r_ap1{k}")
        rb = sid(f"r_ap2{k}", 2)
        got(ra + 1, ap1.at[k, 1])
        pb[hf, xup, 32:64, :] = (p32[hf, xup, 32:64, :] + ap1[k, 1].astype(F32)).astype(BF16)
        go(f"ap2a{k}", rb, pb.at[hf, xup], ap2.at[k, 0], dev(xx=xup))
        got(ra, ap1.at[k, 0])
        pb[hf, xdn, 0:32, :] = (p32[hf, xdn, 0:32, :] + ap1[k, 0].astype(F32)).astype(BF16)
        go(f"ap2b{k}", rb + 1, pb.at[hf, xdn], ap2.at[k, 1], dev(xx=xdn))

    for hf in range(2):
        @pl.loop(0, ROWS // 128)
        def _(i):
            t = pl.ds(pl.multiple_of(i * 128, 128), 128)
            ht[hf, t, :] = hb[hf, :, t].astype(F32).T.astype(BF16)

    def quad_send(k):
        r0, n = CHUNKS[k]
        rows = pl.ds(r0, n)
        for i in range(2):
            got(sid(f"r_yr{k}") + i, yrecv.at[i, rows])
        got(sid(f"r_yo{k}"), yown.at[rows], jnp.logical_not(own))
        when(own, own_local[k].wait)

        @pl.loop(0, n // 128)
        def _(i):
            t = pl.ds(pl.multiple_of(r0 + i * 128, 128), 128)
            v = yown[t, :].astype(F32) + yrecv[0, t, :].astype(F32) + yrecv[1, t, :].astype(F32)
            tt[:, :, t] = v.T.astype(BF16).reshape(4, 64, 128)

        rq = sid(f"r_q{k}", 3)
        for m in (1, 2, 3):
            pm = lax.rem(p + m, 4)
            go(f"q{k}{m}", rq + m - 1, tt.at[pm, :, rows], q1r.at[m - 1, :, rows], dev(zz=4 * q + pm))

    quad_send(0)

    def finish_out(k):
        hf = halves[k]
        rb = sid(f"r_ap2{k}")
        got(rb, ap2.at[k, 0])
        got(rb + 1, ap2.at[k, 1])
        return p32[hf, x] + ap2[k, 0].astype(F32) + ap2[k, 1].astype(F32)

    zsend[...] = finish_out(0).astype(BF16)
    go("z", sid("r_z"), zsend, zrecv, dev(hh=1 - zh))
    xown[...] = finish_out(1)

    quad_send(1)

    def far_send(k):
        r0, n = CHUNKS[k]
        rows = pl.ds(r0, n)
        rq = sid(f"r_q{k}")
        for m in (1, 2, 3):
            got(rq + m - 1, q1r.at[m - 1, :, rows])
        v = tt[p, :, r0:r0 + n].astype(F32)
        for m in range(3):
            v = v + q1r[m, :, r0:r0 + n].astype(F32)
        qs[:, :, r0:r0 + n] = v.astype(BF16).reshape(2, 32, n)
        rn = sid(f"r_near{k}")
        rf = sid(f"r_far{k}")
        go(f"near{k}", rn, qs.at[o, :, rows], near.at[:, rows], other, is_near)
        for c in range(2):
            go(f"far{k}{c}", rf, qs.at[c, :, rows], far.at[:, rows], dev(zz=zfar, cc=c), jnp.logical_not(is_near))

        @pl.when(is_near)
        def _():
            near[:, r0:r0 + n] = qs[s, :, r0:r0 + n]

    far_send(0)
    far_send(1)

    lr.wait()
    lc.wait()
    got(sid("r_z"), zrecv)
    scale = gain[s]
    xin = rv[...].astype(F32) + (xown[...] + zrecv[...].astype(F32)) * MULT
    dz = cv[...].astype(F32) * scale
    sq = jnp.sum(xin * xin, axis=-1, keepdims=True)
    cr = jnp.sum(dz * xin, axis=-1, keepdims=True)
    xown[...] = xin
    stat_out[0] = jnp.broadcast_to(sq, (64, 128))
    stat_out[1] = jnp.broadcast_to(cr, (64, 128))
    go("stat", sid("r_stat"), stat_out, stat_in, other)
    got(sid("r_stat"), stat_in)
    mean_sq = (stat_out[0, :, 0:1] + stat_in[0, :, 0:1]) / FEATURES
    inner_mean = (stat_out[1, :, 0:1] + stat_in[1, :, 0:1]) / FEATURES
    root_inv = lax.rsqrt(mean_sq + 1e-05)
    xin = xown[...]
    dz = cv[...].astype(F32) * scale
    sb[zh, x] = (root_inv * (dz - xin * (inner_mean * root_inv * root_inv))).astype(BF16)
    go("zs", sid("r_zs"), sb.at[zh, x], sb.at[zh, x], dev(hh=1 - zh))

    def spread(k, hf):
        rs = sid(f"r_s{k}", 4)
        go(f"su{k}", rs, sb.at[hf, x], sb.at[hf, x], dev(xx=xup))
        go(f"sd{k}", rs + 1, sb.at[hf, x], sb.at[hf, x], dev(xx=xdn))

    def relay(k, hf):
        rs = sid(f"r_s{k}")
        got(rs + 1, sb.at[hf, xup])
        go(f"fd{k}", rs + 3, sb.at[hf, xup, pl.ds(32, 32)], sb.at[hf, xup, pl.ds(32, 32)], dev(xx=xdn))
        got(rs, sb.at[hf, xdn])
        go(f"fu{k}", rs + 2, sb.at[hf, xdn, pl.ds(0, 32)], sb.at[hf, xdn, pl.ds(0, 32)], dev(xx=xup))

    def relayed(k, hf):
        rs = sid(f"r_s{k}")
        got(rs + 2, sb.at[hf, xfar, pl.ds(0, 32)])
        got(rs + 3, sb.at[hf, xfar, pl.ds(32, 32)])

    spread(0, zh)
    nout[...] = (xin * root_inv * scale).astype(BF16)
    ln = local_copy(nout, normed_hbm)
    ln.start()

    la.wait()
    lm.wait()

    def update(k):
        r0, n = CHUNKS[k]
        rows = pl.ds(r0, n)
        cut = slice(r0, r0 + n)
        got(sid(f"r_near{k}"), near.at[:, rows], jnp.logical_not(is_near))
        got(sid(f"r_far{k}"), far.at[:, rows])
        total = near[:, cut].astype(F32) + far[:, cut].astype(F32)
        anchor = atv[:, cut].astype(F32)
        pseudo = anchor - total / REPLICAS
        moment = (outer_mu * mtv[:, cut].astype(F32) + pseudo).astype(BF16)
        mo[:, cut] = moment
        fresh = (anchor - outer_rate * (pseudo + outer_mu * moment.astype(F32))).astype(BF16)
        nown[:, cut] = fresh
        rt = sid(f"r_ta{k}", 2)
        go(f"tf{k}", rt + s, nown.at[:, rows], ta.at[p, s, :, rows], dev(zz=zfar, cc=q))
        go(f"tn{k}", rt + s, nown.at[:, rows], ta.at[p, s, :, rows], other, jnp.logical_not(is_near))

        @pl.when(is_near)
        def _():
            ta[p, s, :, cut] = fresh

    update(0)
    update(1)
    lo = local_copy(mo, mout_hbm)
    lo.start()

    def quad_gather(k):
        r0, n = CHUNKS[k]
        rows = pl.ds(r0, n)
        rt = sid(f"r_ta{k}")
        for c in range(2):
            got(rt + c, ta.at[p, c, :, rows], jnp.logical_not(jnp.logical_and(is_near, s == c)))
        rg = sid(f"r_g{k}", 3)
        for m in (1, 2, 3):
            pm = lax.rem(p + m, 4)
            go(f"g{k}{m}", rg + m - 1, ta.at[p, :, :, rows], ta.at[p, :, :, rows], dev(zz=4 * q + pm))

    quad_gather(0)
    quad_gather(1)
    relay(0, zh)

    def row_gather(k):
        r0, n = CHUNKS[k]
        rows = pl.ds(r0, n)
        rg = sid(f"r_g{k}")
        for m in (1, 2, 3):
            got(rg + m - 1, ta.at[lax.rem(p + 4 - m, 4), :, :, rows])

        @pl.loop(0, n // 128)
        def _(i):
            t = pl.ds(pl.multiple_of(r0 + i * 128, 128), 128)
            v = ta[:, :, :, t].reshape(256, 128).astype(F32).T.astype(BF16)
            na[t, :] = v

            @pl.when(own)
            def _():
                nfull[t, wcols(je, s)] = v

        ro = sid(f"r_no{k}", 2)
        re = sid(f"r_ne{k}", 2)
        dst = nfull.at[rows, wcols(je, s)]
        go(f"nu{k}", ro + s, na.at[rows], dst, dev(yy=yup, cc=sy))
        go(f"nd{k}", ro + s, na.at[rows], dst, dev(yy=ydn, cc=sy))
        go(f"nn{k}", re + s, na.at[rows], dst, other, jnp.logical_not(own))

    row_gather(0)
    row_gather(1)

    relayed(0, zh)
    shrink = mix_share * STEP * MULT

    @pl.loop(0, COLS // 256)
    def _(i):
        cols = pl.ds(lane(i * 256), 256)
        g = jnp.dot(ht[zh], sb[zh, :, :, cols].reshape(256, 256), preferred_element_type=F32)
        base[:, cols] = mix_share * wv[:, cols].astype(F32) - shrink * g

    got(sid("r_zs"), sb.at[1 - zh, x])
    spread(1, 1 - zh)

    def row_relay(k):
        r0, n = CHUNKS[k]
        rows = pl.ds(r0, n)
        ro = sid(f"r_no{k}")
        for h in range(2):
            got(ro + h, nfull.at[rows, wcols(jo, h)])
        part = nfull.at[rows, wcols(jo, hc)]
        go(f"nf{k}", sid(f"r_ne{k}") + hc, part, part, dev(yy=yo))

    row_relay(0)
    relay(1, 1 - zh)
    row_relay(1)
    relayed(1, 1 - zh)

    for k, (r0, n) in enumerate(CHUNKS):
        re = sid(f"r_ne{k}")
        for h in range(2):
            got(re + h, nfull.at[pl.ds(r0, n), wcols(je, h)], jnp.logical_not(jnp.logical_and(own, s == h)))

    outs = []
    for i in range(COLS // 256):
        cols = pl.ds(i * 256, 256)
        g = jnp.dot(ht[1 - zh], sb[1 - zh, :, :, cols].reshape(256, 256), preferred_element_type=F32)
        mix[:, cols] = (base[:, cols] - shrink * g + (1.0 - mix_share) * nfull[:, cols].astype(F32)).astype(BF16)
        d = local_copy(mix.at[:, cols], mixed_hbm.at[:, cols])
        d.start()
        outs.append(d)
    for cond, d in pending:
        when(cond, d.wait_send)
    ln.wait()
    lo.wait()
    for d in outs:
        d.wait()


def local(hidden_act, residual_in, cotangent, norm_gain, inner_weight, anchor, momentum):
    hbm = pl.BlockSpec(memory_space=pl.ANY)
    vmem = pl.BlockSpec(memory_space=pltpu.VMEM)
    gain = norm_gain.astype(F32).reshape(2, 1, COLS)
    b16 = lambda *shape: pltpu.VMEM(shape, BF16)
    f32 = lambda *shape: pltpu.VMEM(shape, F32)
    normed, mixed, moment = pl.pallas_call(
        kernel,
        out_shape=(
            jax.ShapeDtypeStruct((64, COLS), BF16),
            jax.ShapeDtypeStruct((ROWS, COLS), BF16),
            jax.ShapeDtypeStruct((32, ROWS), BF16),
        ),
        in_specs=[hbm, hbm, hbm, vmem, hbm, hbm, hbm],
        out_specs=(hbm, hbm, hbm),
        scratch_shapes=[
            b16(ROWS, COLS), b16(2, 256, ROWS), b16(2, ROWS, 256), f32(2, 4, 64, COLS), b16(2, 4, 64, COLS),
            b16(2, 2, 32, COLS), b16(2, 2, 64, COLS), f32(64, COLS), b16(64, COLS), b16(64, COLS),
            b16(64, COLS), b16(64, COLS), f32(2, 64, 128), f32(2, 64, 128), b16(2, 4, 64, COLS), b16(64, COLS),
            b16(ROWS, 256), b16(ROWS, 256), b16(2, ROWS, 256), b16(ROWS, 256), b16(4, 64, ROWS),
            b16(3, 64, ROWS), b16(2, 32, ROWS), b16(32, ROWS), b16(32, ROWS), b16(32, ROWS), b16(32, ROWS),
            b16(32, ROWS), b16(32, ROWS), b16(4, 2, 32, ROWS), b16(ROWS, 256), b16(ROWS, COLS),
            f32(ROWS, COLS), b16(ROWS, COLS),
            pltpu.SemaphoreType.DMA((NSEM,)), pltpu.SemaphoreType.DMA((NSEM,)), pltpu.SemaphoreType.DMA((24,)),
        ],
        compiler_params=pltpu.CompilerParams(
            collective_id=0, has_side_effects=True, vmem_limit_bytes=56 * 1024 * 1024
        ),
    )(hidden_act, residual_in, cotangent, gain, inner_weight, anchor.T, momentum.T)
    return (normed, mixed, moment.T)


def solution(mesh):
    in_specs = (
        P("replica", "tensor"),
        P("tensor", "replica"),
        P("tensor", "replica"),
        P(),
        P("tensor", "replica"),
        P("tensor", "replica"),
        P("tensor", "replica"),
    )
    out_specs = (P("tensor", "replica"), P("tensor", "replica"), P("tensor", "replica"))
    return jax.shard_map(local, mesh=mesh, in_specs=in_specs, out_specs=out_specs, check_vma=False)
```

```python
import math

import jax
import jax.numpy as jnp
from jax import lax
from jax.experimental import pallas as pl
from jax.experimental.pallas import tpu as pltpu
from jax.sharding import PartitionSpec as P

FF = 7168
TOK = 512

inner_rate = 0.2
outer_rate = 0.7
outer_mu = 0.9
mix_share = 0.5

F32 = jnp.float32
BF16 = jnp.bfloat16
ROWS = 896
COLS = 1024
CHUNKS = ((0, 256), (256, 256), (512, 256), (768, 128))
NCH = len(CHUNKS)
PIECES = 2
PIECE = 64 // PIECES
MIXCOLS = 256
VMEM_LIMIT = 28 * 1024 * 1024
REPLICAS = 32
FEATURES = 2048
MULT = 1.0 / math.sqrt(FF)
STEP = inner_rate * math.sqrt(FF / TOK)
NSEM = 160


def kernel(
    h_hbm, r_hbm, c_hbm, gain16, w_hbm, at_hbm, mt_hbm,
    normed_hbm, mout_hbm, ht_hbm, sb, nfull,
    wv, hb, ht, p32, pb, ap1, ap2, xown, zsend, zrecv, rv, cv, stat_out, stat_in, slope, nout, gain,
    p1buf, cbuf, yrecv, yown, tt, q1r, qs, near, far, atv, mtv, nown, mo, ta, na,
    send, recv, loc,
):
    ri = lax.axis_index("replica")
    ti = lax.axis_index("tensor")
    s = lax.rem(ri, 2)
    chip = lax.div(ri, 2)
    z = lax.rem(chip, 8)
    y = lax.div(chip, 8)
    zh = lax.div(ti, 4)
    x = lax.rem(ti, 4)
    q = lax.div(z, 4)
    p = lax.rem(z, 4)
    zfar = 4 * (1 - q) + p
    o = 1 - s
    sy = lax.div(y, 2)
    je = lax.rem(y, 2)
    jo = 1 - je
    yb = 2 * s + jo
    plus = lax.rem(yb - y + 4, 4) == 1
    hc = jnp.where(plus, 1, 0)
    hd = 1 - hc
    side = 1 - hc
    yo = lax.rem(2 * y - yb + 4, 4)
    yup = lax.rem(y + 1, 4)
    ydn = lax.rem(y + 3, 4)
    xup = lax.rem(x + 1, 4)
    xdn = lax.rem(x + 3, 4)
    xfar = lax.rem(x + 2, 4)
    own = s == sy
    is_near = s == q

    def dev(yy=y, zz=z, cc=s, hh=zh, xx=x):
        return ((yy * 8 + zz) * 2 + cc, hh * 4 + xx)

    ids = {}
    used = [0, 0]

    def sid(name, count=1):
        if name not in ids:
            kind = name[0][0] == "r"
            ids[name] = used[kind]
            used[kind] += count
            assert used[kind] <= NSEM
        return ids[name]

    pending = []

    def when(cond, f):
        if cond is None:
            f()
        else:
            pl.when(cond)(f)

    other = dev(cc=o)

    def go(sname, ridx, src, dst, device, cond=None):
        d = pltpu.make_async_remote_copy(
            src_ref=src, dst_ref=dst, send_sem=send.at[sid(("s",) + sname)], recv_sem=recv.at[ridx],
            device_id=device, device_id_type=pl.DeviceIdType.MESH,
        )
        when(cond, d.start)
        pending.append((cond, d))

    def got(ridx, dst, cond=None):
        d = pltpu.make_async_remote_copy(
            src_ref=dst, dst_ref=dst, send_sem=send.at[0], recv_sem=recv.at[ridx],
            device_id=other, device_id_type=pl.DeviceIdType.MESH,
        )
        when(cond, d.wait_recv)

    nloc = [0]

    def local_copy(src, dst):
        d = pltpu.make_async_copy(src, dst, loc.at[nloc[0]])
        nloc[0] += 1
        return d

    peers = [other, dev(xx=xup), dev(xx=xdn), dev(hh=1 - zh)]
    for yy in (yup, ydn):
        peers += [dev(yy=yy, cc=0), dev(yy=yy, cc=1)]
    for k in (1, 2, 3):
        peers.append(dev(zz=4 * q + lax.rem(p + k, 4)))
    peers += [dev(zz=zfar, cc=0), dev(zz=zfar, cc=1)]
    lw = local_copy(w_hbm, wv)
    lh = local_copy(h_hbm, hb.at[s])
    lr = local_copy(r_hbm, rv)
    lc = local_copy(c_hbm, cv)
    la = local_copy(at_hbm, atv)
    lm = local_copy(mt_hbm, mtv)
    for d in (lh, lw, lr, lc, la, lm):
        d.start()
    barrier = pltpu.get_barrier_semaphore()
    for peer in peers:
        pl.semaphore_signal(barrier, inc=1, device_id=peer, device_id_type=pl.DeviceIdType.MESH)

    def lane(value):
        return pl.multiple_of(value, 256)

    def wcols(j, h):
        return pl.ds(lane(j * 512 + h * 256), 256)

    def hidden_send():
        go(("h",), sid(("r_h",)), h_hbm, hb.at[s], other)

    own_local = {}

    def far_block(k):
        r0, n = CHUNKS[k]
        rows = pl.ds(r0, n)
        rp1 = sid(("r_p1", k))
        go(("p1a", k), rp1, w_hbm.at[rows, wcols(je, 0)], p1buf.at[rows], dev(yy=ydn), jnp.logical_not(own))
        go(("p1b", k), rp1, w_hbm.at[rows, wcols(je, 1)], p1buf.at[rows], dev(yy=yup), jnp.logical_not(own))
        go(("yo", k), sid(("r_yo", k)), w_hbm.at[rows, wcols(je, o)], yown.at[rows], other, own)
        d = local_copy(w_hbm.at[rows, wcols(je, s)], yown.at[rows])
        when(own, d.start)
        own_local[k] = d

    def direct_half(k):
        r0, n = CHUNKS[k]
        rows = pl.ds(r0, n)
        ryr = sid(("r_yr", k), 2)
        go(("yd", k), ryr + side, w_hbm.at[rows, wcols(jo, hd)], yrecv.at[side, rows], dev(yy=yb, cc=hd))

    def partial_out(half):
        @pl.loop(0, COLS // 256)
        def _(i):
            cols = pl.ds(lane(i * 256), 256)
            v = jnp.dot(hb[half], wv[:, cols], preferred_element_type=F32).reshape(4, 64, 256)
            p32[half, :, :, cols] = v
            pb[half, :, :, cols] = v.astype(BF16)

    def first_out():
        lh.wait()
        lw.wait()
        partial_out(s)

    def second_out():
        got(sid(("r_h",)), hb.at[o])
        partial_out(o)

    halves = (1 - zh, zh)

    def x_far(k, j):
        hf = halves[k]
        ra = sid(("r_ap1", k, j), 2)
        for h, target in ((0, xdn), (1, xup)):
            part = pl.ds(PIECE * j + h * (PIECE // 2), PIECE // 2)
            go(("ap1", k, j, h), ra + h, pb.at[hf, xfar, part], ap1.at[k, j, h], dev(xx=target))

    def combine(k):
        r0, n = CHUNKS[k]
        rows = pl.ds(r0, n)
        got(sid(("r_p1", k)), p1buf.at[rows])

        @pl.loop(0, n // 128)
        def _(i):
            t = pl.ds(pl.multiple_of(r0 + i * 128, 128), 128)
            cbuf[t, :] = (wv[t, wcols(jo, hc)].astype(F32) + p1buf[t, :].astype(F32)).astype(BF16)

        go(("yc", k), sid(("r_yr", k)) + side, cbuf.at[rows], yrecv.at[side, rows], dev(yy=yb, cc=hc))

    def x_near(k, j):
        hf = halves[k]
        ra = sid(("r_ap1", k, j))
        rb = sid(("r_ap2", k, j), 2)
        part = pl.ds(PIECE * j, PIECE)
        for h, target in ((1, xup), (0, xdn)):
            got(ra + h, ap1.at[k, j, h])
            r0 = PIECE * j + h * (PIECE // 2)
            r1 = r0 + PIECE // 2
            pb[hf, target, r0:r1, :] = (p32[hf, target, r0:r1, :] + ap1[k, j, h].astype(F32)).astype(BF16)
            go(("ap2", k, j, h), rb + 1 - h, pb.at[hf, target, part], ap2.at[k, j, 1 - h], dev(xx=target))

    def turn_hidden():
        for hf in range(2):
            @pl.loop(0, ROWS // 128)
            def _(i):
                t = pl.ds(pl.multiple_of(i * 128, 128), 128)
                ht[hf, t, :] = hb[hf, :, t].astype(F32).T.astype(BF16)
        lt.start()

    def quad_send(k):
        r0, n = CHUNKS[k]
        rows = pl.ds(r0, n)
        for i in range(2):
            got(sid(("r_yr", k)) + i, yrecv.at[i, rows])
        got(sid(("r_yo", k)), yown.at[rows], jnp.logical_not(own))
        when(own, own_local[k].wait)

        @pl.loop(0, n // 128)
        def _(i):
            t = pl.ds(pl.multiple_of(r0 + i * 128, 128), 128)
            v = yown[t, :].astype(F32) + yrecv[0, t, :].astype(F32) + yrecv[1, t, :].astype(F32)
            tt[:, :, t] = v.T.astype(BF16).reshape(4, 64, 128)

        rq = sid(("r_q", k), 3)
        for m in (1, 2, 3):
            pm = lax.rem(p + m, 4)
            go(("q", k, m), rq + m - 1, tt.at[pm, :, rows], q1r.at[m - 1, :, rows], dev(zz=4 * q + pm))

    def finish_out(k, j):
        hf = halves[k]
        rb = sid(("r_ap2", k, j))
        got(rb, ap2.at[k, j, 0])
        got(rb + 1, ap2.at[k, j, 1])
        v = p32[hf, x, PIECE * j:PIECE * (j + 1), :]
        return v + ap2[k, j, 0].astype(F32) + ap2[k, j, 1].astype(F32)

    def z_send(j):
        zsend[j] = finish_out(0, j).astype(BF16)
        go(("z", j), sid(("r_z", j)), zsend.at[j], zrecv.at[j], dev(hh=1 - zh))

    def x_own(j):
        xown[j] = finish_out(1, j)

    def far_send(k):
        r0, n = CHUNKS[k]
        rows = pl.ds(r0, n)
        rq = sid(("r_q", k))
        for m in (1, 2, 3):
            got(rq + m - 1, q1r.at[m - 1, :, rows])
        v = tt[p, :, r0:r0 + n].astype(F32)
        for m in range(3):
            v = v + q1r[m, :, r0:r0 + n].astype(F32)
        qs[:, :, r0:r0 + n] = v.astype(BF16).reshape(2, 32, n)
        rn = sid(("r_near", k))
        rf = sid(("r_far", k))
        go(("near", k), rn, qs.at[o, :, rows], near.at[:, rows], other, is_near)
        for c in range(2):
            go(("far", k, c), rf, qs.at[c, :, rows], far.at[:, rows], dev(zz=zfar, cc=c), jnp.logical_not(is_near))

        @pl.when(is_near)
        def _():
            near[:, r0:r0 + n] = qs[s, :, r0:r0 + n]

    def stats(j):
        if j == 0:
            lr.wait()
            lc.wait()
        part = slice(PIECE * j, PIECE * (j + 1))
        got(sid(("r_z", j)), zrecv.at[j])
        xin = rv[part, :].astype(F32) + (xown[j] + zrecv[j].astype(F32)) * MULT
        dz = cv[part, :].astype(F32) * gain[...]
        xown[j] = xin
        stat_out[j, 0] = jnp.broadcast_to(jnp.sum(xin * xin, axis=-1, keepdims=True), (PIECE, 128))
        stat_out[j, 1] = jnp.broadcast_to(jnp.sum(dz * xin, axis=-1, keepdims=True), (PIECE, 128))
        go(("stat", j), sid(("r_stat", j)), stat_out.at[j], stat_in.at[j], other)

    def norm(j):
        part = slice(PIECE * j, PIECE * (j + 1))
        rows = pl.ds(PIECE * j, PIECE)
        got(sid(("r_stat", j)), stat_in.at[j])
        mean_sq = (stat_out[j, 0, :, 0:1] + stat_in[j, 0, :, 0:1]) / FEATURES
        inner_mean = (stat_out[j, 1, :, 0:1] + stat_in[j, 1, :, 0:1]) / FEATURES
        root_inv = lax.rsqrt(mean_sq + 1e-05)
        xin = xown[j]
        dz = cv[part, :].astype(F32) * gain[...]
        slope[part, :] = (root_inv * (dz - xin * (inner_mean * root_inv * root_inv))).astype(BF16)
        go(("zs", j), sid(("r_zs", j)), slope.at[rows], sb.at[zh, x, rows], dev(hh=1 - zh))
        spread(0, j, slope.at[rows])
        nout[part, :] = (xin * root_inv * gain[...]).astype(BF16)
        if j == PIECES - 1:
            ln.start()
            ls.start()

    def spread(k, j, src):
        rs = sid(("r_s", k, j), 4)
        dst = sb.at[(zh, 1 - zh)[k], x, pl.ds(PIECE * j, PIECE)]
        go(("su", k, j), rs, src, dst, dev(xx=xup))
        go(("sd", k, j), rs + 1, src, dst, dev(xx=xdn))

    def relay(k, j):
        rs = sid(("r_s", k, j))
        hf = (zh, 1 - zh)[k]
        for h, source, target in ((1, xup, xdn), (0, xdn, xup)):
            got(rs + h, sb.at[hf, source, pl.ds(PIECE * j, PIECE)])
            part = sb.at[hf, source, pl.ds(PIECE * j + h * (PIECE // 2), PIECE // 2)]
            go(("f", k, j, h), rs + 2 + h, part, part, dev(xx=target))

    def relayed(k, j):
        rs = sid(("r_s", k, j))
        for h in range(2):
            got(rs + 2 + h, sb.at[(zh, 1 - zh)[k], xfar, pl.ds(PIECE * j + h * (PIECE // 2), PIECE // 2)])

    def update(k):
        if k == 0:
            la.wait()
            lm.wait()
        r0, n = CHUNKS[k]
        rows = pl.ds(r0, n)
        cut = slice(r0, r0 + n)
        got(sid(("r_near", k)), near.at[:, rows], jnp.logical_not(is_near))
        got(sid(("r_far", k)), far.at[:, rows])
        total = near[:, cut].astype(F32) + far[:, cut].astype(F32)
        anchor = atv[:, cut].astype(F32)
        pseudo = anchor - total / REPLICAS
        moment = (outer_mu * mtv[:, cut].astype(F32) + pseudo).astype(BF16)
        mo[:, cut] = moment
        fresh = (anchor - outer_rate * (pseudo + outer_mu * moment.astype(F32))).astype(BF16)
        nown[:, cut] = fresh
        rt = sid(("r_ta", k), 2)
        go(("tf", k), rt + s, nown.at[:, rows], ta.at[p, s, :, rows], dev(zz=zfar, cc=q))
        go(("tn", k), rt + s, nown.at[:, rows], ta.at[p, s, :, rows], other, jnp.logical_not(is_near))

        @pl.when(is_near)
        def _():
            ta[p, s, :, cut] = fresh

        if k == NCH - 1:
            lo.start()

    def quad_gather(k):
        r0, n = CHUNKS[k]
        rows = pl.ds(r0, n)
        rt = sid(("r_ta", k))
        for c in range(2):
            got(rt + c, ta.at[p, c, :, rows], jnp.logical_not(jnp.logical_and(is_near, s == c)))
        rg = sid(("r_g", k), 3)
        for m in (1, 2, 3):
            pm = lax.rem(p + m, 4)
            go(("g", k, m), rg + m - 1, ta.at[p, :, :, rows], ta.at[p, :, :, rows], dev(zz=4 * q + pm))

    def row_gather(k):
        r0, n = CHUNKS[k]
        rows = pl.ds(r0, n)
        rg = sid(("r_g", k))
        for m in (1, 2, 3):
            got(rg + m - 1, ta.at[lax.rem(p + 4 - m, 4), :, :, rows])

        @pl.loop(0, n // 128)
        def _(i):
            t = pl.ds(pl.multiple_of(r0 + i * 128, 128), 128)
            na[t, :] = ta[:, :, :, t].reshape(256, 128).astype(F32).T.astype(BF16)

        ro = sid(("r_no", k), 2)
        re = sid(("r_ne", k), 2)
        dst = nfull.at[rows, wcols(je, s)]
        go(("nu", k), ro + s, na.at[rows], dst, dev(yy=yup, cc=sy))
        go(("nd", k), ro + s, na.at[rows], dst, dev(yy=ydn, cc=sy))
        go(("nn", k), re + s, na.at[rows], dst, other, jnp.logical_not(own))
        d = local_copy(na.at[rows], dst)
        when(own, d.start)
        own_out.append(d)

    def z_spread(j):
        part = sb.at[1 - zh, x, pl.ds(PIECE * j, PIECE)]
        got(sid(("r_zs", j)), part)
        spread(1, j, part)

    def row_relay(k):
        r0, n = CHUNKS[k]
        rows = pl.ds(r0, n)
        ro = sid(("r_no", k))
        for h in range(2):
            got(ro + h, nfull.at[rows, wcols(jo, h)])
        part = nfull.at[rows, wcols(jo, hc)]
        go(("nf", k), sid(("r_ne", k)) + hc, part, part, dev(yy=yo))

    def row_done(k):
        r0, n = CHUNKS[k]
        re = sid(("r_ne", k))
        for h in range(2):
            got(re + h, nfull.at[pl.ds(r0, n), wcols(je, h)], jnp.logical_not(jnp.logical_and(own, s == h)))

    ln = local_copy(nout, normed_hbm)
    lo = local_copy(mo, mout_hbm)
    ls = local_copy(slope, sb.at[zh, x])
    lt = local_copy(ht, ht_hbm)
    own_out = []

    def enter():
        pl.semaphore_wait(barrier, len(peers))

    def gain_row():
        v = gain16[pl.ds(pl.multiple_of(8 * s, 8), 8), :].astype(F32)
        for i in range(8):
            gain[:, 128 * i:128 * (i + 1)] = v[i:i + 1, :]

    steps = (
        (first_out,), (gain_row,), (enter,), (hidden_send,), (far_block, 0), (direct_half, 0), (far_block, 1),
        (second_out,), (x_far, 0, 0), (x_far, 0, 1), (x_far, 1, 0), (x_far, 1, 1), (combine, 0), (direct_half, 1),
        (far_block, 2), (x_near, 0, 0), (x_near, 0, 1), (combine, 1), (direct_half, 2), (far_block, 3),
        (quad_send, 0), (x_near, 1, 0), (x_near, 1, 1), (combine, 2), (direct_half, 3), (z_send, 0), (z_send, 1),
        (combine, 3), (quad_send, 1), (far_send, 0), (x_own, 0), (x_own, 1), (quad_send, 2), (far_send, 1),
        (update, 0), (quad_send, 3), (far_send, 2), (update, 1), (quad_gather, 0), (turn_hidden,), (far_send, 3),
        (update, 2), (quad_gather, 1), (row_gather, 0), (stats, 0), (norm, 0), (stats, 1), (norm, 1), (update, 3),
        (quad_gather, 2), (row_gather, 1), (quad_gather, 3), (relay, 0, 0), (relay, 0, 1), (row_relay, 0),
        (row_gather, 2), (row_relay, 1), (z_spread, 0), (z_spread, 1), (row_gather, 3), (relayed, 0, 0),
        (relayed, 0, 1), (row_relay, 2), (relay, 1, 0), (relay, 1, 1), (row_relay, 3), (relayed, 1, 0),
        (relayed, 1, 1), (row_done, 0), (row_done, 1), (row_done, 2), (row_done, 3),
    )
    for step, *args in steps:
        step(*args)
    for cond, d in pending:
        when(cond, d.wait_send)
    for d in (ln, lo, ls, lt):
        d.wait()
    for d in own_out:
        when(own, d.wait)


def mix_kernel(ht, sb, w, n, normed_in, mout_in, mixed, normed_out, mout_out, sem):
    i = pl.program_id(0)
    shrink = mix_share * STEP * MULT
    copies = (
        pltpu.make_async_copy(normed_in, normed_out, sem.at[0]),
        pltpu.make_async_copy(mout_in, mout_out, sem.at[1]),
    )

    @pl.when(i == 0)
    def _():
        for d in copies:
            d.start()

    g = jnp.dot(ht[0], sb[0].reshape(256, MIXCOLS), preferred_element_type=F32)
    g = g + jnp.dot(ht[1], sb[1].reshape(256, MIXCOLS), preferred_element_type=F32)
    mixed[...] = (mix_share * w[...].astype(F32) - shrink * g + (1.0 - mix_share) * n[...].astype(F32)).astype(BF16)

    @pl.when(i == pl.num_programs(0) - 1)
    def _():
        for d in copies:
            d.wait()


def local(hidden_act, residual_in, cotangent, norm_gain, inner_weight, anchor, momentum):
    hbm = pl.BlockSpec(memory_space=pl.ANY)
    away = pl.BlockSpec(memory_space=pltpu.HBM)
    vmem = pl.BlockSpec(memory_space=pltpu.VMEM)
    b16 = lambda *shape: pltpu.VMEM(shape, BF16)
    f32 = lambda *shape: pltpu.VMEM(shape, F32)
    stay = lambda v: pltpu.with_memory_space_constraint(v, pltpu.HBM)
    like = lambda *shape: jax.ShapeDtypeStruct(shape, BF16)
    normed, moment, ht, sb, nfull = pl.pallas_call(
        kernel,
        out_shape=(like(64, COLS), like(32, ROWS), like(2, ROWS, 256), like(2, 4, 64, COLS), like(ROWS, COLS)),
        in_specs=[away, away, away, vmem, away, away, away],
        out_specs=(hbm,) * 5,
        scratch_shapes=[
            b16(ROWS, COLS), b16(2, 256, ROWS), b16(2, ROWS, 256), f32(2, 4, 64, COLS), b16(2, 4, 64, COLS),
            b16(2, PIECES, 2, PIECE // 2, COLS), b16(2, PIECES, 2, PIECE, COLS), f32(PIECES, PIECE, COLS),
            b16(PIECES, PIECE, COLS), b16(PIECES, PIECE, COLS), b16(64, COLS), b16(64, COLS),
            f32(PIECES, 2, PIECE, 128), f32(PIECES, 2, PIECE, 128), b16(64, COLS), b16(64, COLS), f32(1, COLS),
            b16(ROWS, 256), b16(ROWS, 256), b16(2, ROWS, 256), b16(ROWS, 256), b16(4, 64, ROWS),
            b16(3, 64, ROWS), b16(2, 32, ROWS), b16(32, ROWS), b16(32, ROWS), b16(32, ROWS), b16(32, ROWS),
            b16(32, ROWS), b16(32, ROWS), b16(4, 2, 32, ROWS), b16(ROWS, 256),
            pltpu.SemaphoreType.DMA((NSEM,)), pltpu.SemaphoreType.DMA((NSEM,)), pltpu.SemaphoreType.DMA((24,)),
        ],
        compiler_params=pltpu.CompilerParams(
            collective_id=0, has_side_effects=True, vmem_limit_bytes=VMEM_LIMIT
        ),
    )(
        stay(hidden_act), stay(residual_in), stay(cotangent), norm_gain.reshape(16, 128), stay(inner_weight),
        stay(anchor.T), stay(momentum.T),
    )
    column = lambda i: (0, i)
    mixed, normed, moment = pl.pallas_call(
        mix_kernel,
        grid=(COLS // MIXCOLS,),
        out_shape=(like(ROWS, COLS), like(64, COLS), like(32, ROWS)),
        in_specs=[
            pl.BlockSpec((2, ROWS, 256), lambda i: (0, 0, 0)),
            pl.BlockSpec((2, 4, 64, MIXCOLS), lambda i: (0, 0, 0, i)),
            pl.BlockSpec((ROWS, MIXCOLS), column),
            pl.BlockSpec((ROWS, MIXCOLS), column),
            hbm, hbm,
        ],
        out_specs=(pl.BlockSpec((ROWS, MIXCOLS), column), hbm, hbm),
        scratch_shapes=[pltpu.SemaphoreType.DMA((2,))],
        compiler_params=pltpu.CompilerParams(vmem_limit_bytes=24 * 1024 * 1024),
    )(ht, sb, inner_weight, nfull, normed, moment)
    return (normed, mixed, moment.T)


def solution(mesh):
    in_specs = (
        P("replica", "tensor"),
        P("tensor", "replica"),
        P("tensor", "replica"),
        P(),
        P("tensor", "replica"),
        P("tensor", "replica"),
        P("tensor", "replica"),
    )
    out_specs = (P("tensor", "replica"), P("tensor", "replica"), P("tensor", "replica"))
    return jax.shard_map(local, mesh=mesh, in_specs=in_specs, out_specs=out_specs, check_vma=False)
```

```python
import math

import jax
import jax.numpy as jnp
from jax import lax
from jax.experimental import pallas as pl
from jax.experimental.pallas import tpu as pltpu
from jax.sharding import PartitionSpec as P

FF = 7168
TOK = 512

inner_rate = 0.2
outer_rate = 0.7
outer_mu = 0.9
mix_share = 0.5

F32 = jnp.float32
BF16 = jnp.bfloat16
ROWS = 896
COLS = 1024
CHUNKS = ((0, 256), (256, 256), (512, 256), (768, 128))
NCH = len(CHUNKS)
PIECES = 2
PIECE = 64 // PIECES
MIXCOLS = 256
VMEM_LIMIT = 28 * 1024 * 1024
REPLICAS = 32
FEATURES = 2048
MULT = 1.0 / math.sqrt(FF)
STEP = inner_rate * math.sqrt(FF / TOK)
NSEM = 160


def kernel(
    h_hbm, r_hbm, c_hbm, gain16, w_hbm, at_hbm, mt_hbm,
    normed_hbm, mout_hbm, ht_hbm, sb, nfull,
    wv, hb, ht, p32, pb, ap1, ap2, xown, zsend, zrecv, rv, cv, stat_out, stat_in, slope, nout, gain,
    p1buf, cbuf, yrecv, yown, tt, q1r, qs, near, far, atv, mtv, nown, mo, ta, na,
    send, recv, loc,
):
    ri = lax.axis_index("replica")
    ti = lax.axis_index("tensor")
    s = lax.rem(ri, 2)
    chip = lax.div(ri, 2)
    z = lax.rem(chip, 8)
    y = lax.div(chip, 8)
    zh = lax.div(ti, 4)
    x = lax.rem(ti, 4)
    q = lax.div(z, 4)
    p = lax.rem(z, 4)
    zfar = 4 * (1 - q) + p
    o = 1 - s
    sy = lax.div(y, 2)
    je = lax.rem(y, 2)
    jo = 1 - je
    yb = 2 * s + jo
    plus = lax.rem(yb - y + 4, 4) == 1
    hc = jnp.where(plus, 1, 0)
    hd = 1 - hc
    side = 1 - hc
    yo = lax.rem(2 * y - yb + 4, 4)
    yup = lax.rem(y + 1, 4)
    ydn = lax.rem(y + 3, 4)
    xup = lax.rem(x + 1, 4)
    xdn = lax.rem(x + 3, 4)
    xfar = lax.rem(x + 2, 4)
    own = s == sy
    is_near = s == q

    def dev(yy=y, zz=z, cc=s, hh=zh, xx=x):
        return ((yy * 8 + zz) * 2 + cc, hh * 4 + xx)

    ids = {}
    used = [0, 0]

    def sid(name, count=1):
        if name not in ids:
            kind = name[0][0] == "r"
            ids[name] = used[kind]
            used[kind] += count
            assert used[kind] <= NSEM
        return ids[name]

    pending = []

    def when(cond, f):
        if cond is None:
            f()
        else:
            pl.when(cond)(f)

    other = dev(cc=o)

    def go(sname, ridx, src, dst, device, cond=None):
        d = pltpu.make_async_remote_copy(
            src_ref=src, dst_ref=dst, send_sem=send.at[sid(("s",) + sname)], recv_sem=recv.at[ridx],
            device_id=device, device_id_type=pl.DeviceIdType.MESH,
        )
        when(cond, d.start)
        pending.append((cond, d))

    def got(ridx, dst, cond=None):
        d = pltpu.make_async_remote_copy(
            src_ref=dst, dst_ref=dst, send_sem=send.at[0], recv_sem=recv.at[ridx],
            device_id=other, device_id_type=pl.DeviceIdType.MESH,
        )
        when(cond, d.wait_recv)

    nloc = [0]

    def local_copy(src, dst):
        d = pltpu.make_async_copy(src, dst, loc.at[nloc[0]])
        nloc[0] += 1
        return d

    peers = [other, dev(xx=xup), dev(xx=xdn), dev(hh=1 - zh)]
    for yy in (yup, ydn):
        peers += [dev(yy=yy, cc=0), dev(yy=yy, cc=1)]
    for k in (1, 2, 3):
        peers.append(dev(zz=4 * q + lax.rem(p + k, 4)))
    peers += [dev(zz=zfar, cc=0), dev(zz=zfar, cc=1)]
    lw = local_copy(w_hbm, wv)
    lh = local_copy(h_hbm, hb.at[s])
    lr = local_copy(r_hbm, rv)
    lc = local_copy(c_hbm, cv)
    la = local_copy(at_hbm, atv)
    lm = local_copy(mt_hbm, mtv)
    for d in (lh, lw, lr, lc, la, lm):
        d.start()
    barrier = pltpu.get_barrier_semaphore()
    for peer in peers:
        pl.semaphore_signal(barrier, inc=1, device_id=peer, device_id_type=pl.DeviceIdType.MESH)

    def lane(value):
        return pl.multiple_of(value, 256)

    def wcols(j, h):
        return pl.ds(lane(j * 512 + h * 256), 256)

    def hidden_send():
        go(("h",), sid(("r_h",)), h_hbm, hb.at[s], other)

    own_local = {}

    def far_block(k):
        r0, n = CHUNKS[k]
        rows = pl.ds(r0, n)
        rp1 = sid(("r_p1", k))
        go(("p1a", k), rp1, w_hbm.at[rows, wcols(je, 0)], p1buf.at[rows], dev(yy=ydn), jnp.logical_not(own))
        go(("p1b", k), rp1, w_hbm.at[rows, wcols(je, 1)], p1buf.at[rows], dev(yy=yup), jnp.logical_not(own))
        go(("yo", k), sid(("r_yo", k)), w_hbm.at[rows, wcols(je, o)], yown.at[rows], other, own)
        d = local_copy(w_hbm.at[rows, wcols(je, s)], yown.at[rows])
        when(own, d.start)
        own_local[k] = d

    def direct_half(k):
        r0, n = CHUNKS[k]
        rows = pl.ds(r0, n)
        ryr = sid(("r_yr", k), 2)
        go(("yd", k), ryr + side, w_hbm.at[rows, wcols(jo, hd)], yrecv.at[side, rows], dev(yy=yb, cc=hd))

    def partial_out(half):
        @pl.loop(0, COLS // 256)
        def _(i):
            cols = pl.ds(lane(i * 256), 256)
            v = jnp.dot(hb[half], wv[:, cols], preferred_element_type=F32).reshape(4, 64, 256)
            p32[half, :, :, cols] = v
            pb[half, :, :, cols] = v.astype(BF16)

    def first_out():
        lh.wait()
        lw.wait()
        partial_out(s)

    def second_out():
        got(sid(("r_h",)), hb.at[o])
        partial_out(o)

    halves = (1 - zh, zh)

    def x_far(k, j):
        hf = halves[k]
        ra = sid(("r_ap1", k, j), 2)
        for h, target in ((0, xdn), (1, xup)):
            part = pl.ds(PIECE * j + h * (PIECE // 2), PIECE // 2)
            go(("ap1", k, j, h), ra + h, pb.at[hf, xfar, part], ap1.at[k, j, h], dev(xx=target))

    def combine(k):
        r0, n = CHUNKS[k]
        rows = pl.ds(r0, n)
        got(sid(("r_p1", k)), p1buf.at[rows])

        @pl.loop(0, n // 128)
        def _(i):
            t = pl.ds(pl.multiple_of(r0 + i * 128, 128), 128)
            cbuf[t, :] = (wv[t, wcols(jo, hc)].astype(F32) + p1buf[t, :].astype(F32)).astype(BF16)

        go(("yc", k), sid(("r_yr", k)) + side, cbuf.at[rows], yrecv.at[side, rows], dev(yy=yb, cc=hc))

    def x_near(k, j):
        hf = halves[k]
        ra = sid(("r_ap1", k, j))
        rb = sid(("r_ap2", k, j), 2)
        part = pl.ds(PIECE * j, PIECE)
        for h, target in ((1, xup), (0, xdn)):
            got(ra + h, ap1.at[k, j, h])
            r0 = PIECE * j + h * (PIECE // 2)
            r1 = r0 + PIECE // 2
            pb[hf, target, r0:r1, :] = (p32[hf, target, r0:r1, :] + ap1[k, j, h].astype(F32)).astype(BF16)
            go(("ap2", k, j, h), rb + 1 - h, pb.at[hf, target, part], ap2.at[k, j, 1 - h], dev(xx=target))

    def turn_hidden():
        for hf in range(2):
            @pl.loop(0, ROWS // 128)
            def _(i):
                t = pl.ds(pl.multiple_of(i * 128, 128), 128)
                ht[hf, t, :] = hb[hf, :, t].astype(F32).T.astype(BF16)
        lt.start()

    def quad_send(k):
        r0, n = CHUNKS[k]
        rows = pl.ds(r0, n)
        for i in range(2):
            got(sid(("r_yr", k)) + i, yrecv.at[i, rows])
        got(sid(("r_yo", k)), yown.at[rows], jnp.logical_not(own))
        when(own, own_local[k].wait)

        @pl.loop(0, n // 128)
        def _(i):
            t = pl.ds(pl.multiple_of(r0 + i * 128, 128), 128)
            v = yown[t, :].astype(F32) + yrecv[0, t, :].astype(F32) + yrecv[1, t, :].astype(F32)
            tt[:, :, t] = v.T.astype(BF16).reshape(4, 64, 128)

        rq = sid(("r_q", k), 3)
        for m in (1, 2, 3):
            pm = lax.rem(p + m, 4)
            go(("q", k, m), rq + m - 1, tt.at[pm, :, rows], q1r.at[m - 1, :, rows], dev(zz=4 * q + pm))

    def finish_out(k, j):
        hf = halves[k]
        rb = sid(("r_ap2", k, j))
        got(rb, ap2.at[k, j, 0])
        got(rb + 1, ap2.at[k, j, 1])
        v = p32[hf, x, PIECE * j:PIECE * (j + 1), :]
        return v + ap2[k, j, 0].astype(F32) + ap2[k, j, 1].astype(F32)

    def z_send(j):
        zsend[j] = finish_out(0, j).astype(BF16)
        go(("z", j), sid(("r_z", j)), zsend.at[j], zrecv.at[j], dev(hh=1 - zh))

    def x_own(j):
        xown[j] = finish_out(1, j)

    def far_send(k):
        r0, n = CHUNKS[k]
        rows = pl.ds(r0, n)
        rq = sid(("r_q", k))
        for m in (1, 2, 3):
            got(rq + m - 1, q1r.at[m - 1, :, rows])
        v = tt[p, :, r0:r0 + n].astype(F32)
        for m in range(3):
            v = v + q1r[m, :, r0:r0 + n].astype(F32)
        qs[:, :, r0:r0 + n] = v.astype(BF16).reshape(2, 32, n)
        rn = sid(("r_near", k))
        rf = sid(("r_far", k))
        go(("near", k), rn, qs.at[o, :, rows], near.at[:, rows], other, is_near)
        for c in range(2):
            go(("far", k, c), rf, qs.at[c, :, rows], far.at[:, rows], dev(zz=zfar, cc=c), jnp.logical_not(is_near))

        @pl.when(is_near)
        def _():
            near[:, r0:r0 + n] = qs[s, :, r0:r0 + n]

    def stats(j):
        if j == 0:
            lr.wait()
            lc.wait()
        part = slice(PIECE * j, PIECE * (j + 1))
        got(sid(("r_z", j)), zrecv.at[j])
        xin = rv[part, :].astype(F32) + (xown[j] + zrecv[j].astype(F32)) * MULT
        dz = cv[part, :].astype(F32) * gain[...]
        xown[j] = xin
        stat_out[j, 0] = jnp.broadcast_to(jnp.sum(xin * xin, axis=-1, keepdims=True), (PIECE, 128))
        stat_out[j, 1] = jnp.broadcast_to(jnp.sum(dz * xin, axis=-1, keepdims=True), (PIECE, 128))
        go(("stat", j), sid(("r_stat", j)), stat_out.at[j], stat_in.at[j], other)

    def norm(j):
        part = slice(PIECE * j, PIECE * (j + 1))
        rows = pl.ds(PIECE * j, PIECE)
        got(sid(("r_stat", j)), stat_in.at[j])
        mean_sq = (stat_out[j, 0, :, 0:1] + stat_in[j, 0, :, 0:1]) / FEATURES
        inner_mean = (stat_out[j, 1, :, 0:1] + stat_in[j, 1, :, 0:1]) / FEATURES
        root_inv = lax.rsqrt(mean_sq + 1e-05)
        xin = xown[j]
        dz = cv[part, :].astype(F32) * gain[...]
        slope[part, :] = (root_inv * (dz - xin * (inner_mean * root_inv * root_inv))).astype(BF16)
        go(("zs", j), sid(("r_zs", j)), slope.at[rows], sb.at[zh, x, rows], dev(hh=1 - zh))
        spread(0, j, slope.at[rows])
        nout[part, :] = (xin * root_inv * gain[...]).astype(BF16)
        if j == PIECES - 1:
            ln.start()
            ls.start()

    def spread(k, j, src):
        rs = sid(("r_s", k, j), 4)
        dst = sb.at[(zh, 1 - zh)[k], x, pl.ds(PIECE * j, PIECE)]
        go(("su", k, j), rs, src, dst, dev(xx=xup))
        go(("sd", k, j), rs + 1, src, dst, dev(xx=xdn))

    def relay(k, j):
        rs = sid(("r_s", k, j))
        hf = (zh, 1 - zh)[k]
        for h, source, target in ((1, xup, xdn), (0, xdn, xup)):
            got(rs + h, sb.at[hf, source, pl.ds(PIECE * j, PIECE)])
            part = sb.at[hf, source, pl.ds(PIECE * j + h * (PIECE // 2), PIECE // 2)]
            go(("f", k, j, h), rs + 2 + h, part, part, dev(xx=target))

    def relayed(k, j):
        rs = sid(("r_s", k, j))
        for h in range(2):
            got(rs + 2 + h, sb.at[(zh, 1 - zh)[k], xfar, pl.ds(PIECE * j + h * (PIECE // 2), PIECE // 2)])

    def update(k):
        if k == 0:
            la.wait()
            lm.wait()
        r0, n = CHUNKS[k]
        rows = pl.ds(r0, n)
        cut = slice(r0, r0 + n)
        got(sid(("r_near", k)), near.at[:, rows], jnp.logical_not(is_near))
        got(sid(("r_far", k)), far.at[:, rows])
        total = near[:, cut].astype(F32) + far[:, cut].astype(F32)
        anchor = atv[:, cut].astype(F32)
        pseudo = anchor - total / REPLICAS
        moment = (outer_mu * mtv[:, cut].astype(F32) + pseudo).astype(BF16)
        mo[:, cut] = moment
        fresh = (anchor - outer_rate * (pseudo + outer_mu * moment.astype(F32))).astype(BF16)
        nown[:, cut] = fresh
        rt = sid(("r_ta", k), 2)
        go(("tf", k), rt + s, nown.at[:, rows], ta.at[p, s, :, rows], dev(zz=zfar, cc=q))
        go(("tn", k), rt + s, nown.at[:, rows], ta.at[p, s, :, rows], other, jnp.logical_not(is_near))

        @pl.when(is_near)
        def _():
            ta[p, s, :, cut] = fresh

        if k == NCH - 1:
            lo.start()

    def quad_gather(k):
        r0, n = CHUNKS[k]
        rows = pl.ds(r0, n)
        rt = sid(("r_ta", k))
        for c in range(2):
            got(rt + c, ta.at[p, c, :, rows], jnp.logical_not(jnp.logical_and(is_near, s == c)))
        rg = sid(("r_g", k), 3)
        for m in (1, 2, 3):
            pm = lax.rem(p + m, 4)
            go(("g", k, m), rg + m - 1, ta.at[p, :, :, rows], ta.at[p, :, :, rows], dev(zz=4 * q + pm))

    def row_gather(k):
        r0, n = CHUNKS[k]
        rows = pl.ds(r0, n)
        rg = sid(("r_g", k))
        for m in (1, 2, 3):
            got(rg + m - 1, ta.at[lax.rem(p + 4 - m, 4), :, :, rows])

        @pl.loop(0, n // 128)
        def _(i):
            t = pl.ds(pl.multiple_of(r0 + i * 128, 128), 128)
            na[t, :] = ta[:, :, :, t].reshape(256, 128).astype(F32).T.astype(BF16)

        ro = sid(("r_no", k), 2)
        re = sid(("r_ne", k), 2)
        dst = nfull.at[rows, wcols(je, s)]
        go(("nu", k), ro + s, na.at[rows], dst, dev(yy=yup, cc=sy))
        go(("nd", k), ro + s, na.at[rows], dst, dev(yy=ydn, cc=sy))
        go(("nn", k), re + s, na.at[rows], dst, other, jnp.logical_not(own))
        d = local_copy(na.at[rows], dst)
        when(own, d.start)
        own_out.append(d)

    def z_spread(j):
        part = sb.at[1 - zh, x, pl.ds(PIECE * j, PIECE)]
        got(sid(("r_zs", j)), part)
        spread(1, j, part)

    def row_relay(k):
        r0, n = CHUNKS[k]
        rows = pl.ds(r0, n)
        ro = sid(("r_no", k))
        for h in range(2):
            got(ro + h, nfull.at[rows, wcols(jo, h)])
        part = nfull.at[rows, wcols(jo, hc)]
        go(("nf", k), sid(("r_ne", k)) + hc, part, part, dev(yy=yo))

    def row_done(k):
        r0, n = CHUNKS[k]
        re = sid(("r_ne", k))
        for h in range(2):
            got(re + h, nfull.at[pl.ds(r0, n), wcols(je, h)], jnp.logical_not(jnp.logical_and(own, s == h)))

    ln = local_copy(nout, normed_hbm)
    lo = local_copy(mo, mout_hbm)
    ls = local_copy(slope, sb.at[zh, x])
    lt = local_copy(ht, ht_hbm)
    own_out = []

    def enter():
        pl.semaphore_wait(barrier, len(peers))

    def gain_row():
        v = gain16[pl.ds(pl.multiple_of(8 * s, 8), 8), :].astype(F32)
        for i in range(8):
            gain[:, 128 * i:128 * (i + 1)] = v[i:i + 1, :]

    steps = (
        (first_out,), (gain_row,), (enter,), (hidden_send,), (far_block, 0), (direct_half, 0),
        (far_block, 1), (second_out,), (x_far, 0, 0), (x_far, 0, 1), (x_far, 1, 0), (x_far, 1, 1), (combine, 0),
        (direct_half, 1), (far_block, 2), (x_near, 0, 0), (x_near, 0, 1), (combine, 1), (direct_half, 2),
        (far_block, 3), (quad_send, 0), (x_near, 1, 0), (x_near, 1, 1), (combine, 2), (direct_half, 3), (z_send, 0),
        (z_send, 1), (combine, 3), (quad_send, 1), (far_send, 0), (x_own, 0), (x_own, 1), (quad_send, 2),
        (far_send, 1), (update, 0), (quad_send, 3), (far_send, 2), (update, 1), (quad_gather, 0), (turn_hidden,),
        (far_send, 3), (update, 2), (quad_gather, 1), (row_gather, 0), (stats, 0), (update, 3), (norm, 0), (stats, 1),
        (quad_gather, 2), (norm, 1), (row_gather, 1), (quad_gather, 3), (relay, 0, 0), (relay, 0, 1), (row_relay, 0),
        (row_gather, 2), (row_relay, 1), (z_spread, 0), (z_spread, 1), (row_gather, 3), (relayed, 0, 0),
        (relayed, 0, 1), (row_relay, 2), (relay, 1, 0), (relay, 1, 1), (row_relay, 3), (relayed, 1, 0),
        (relayed, 1, 1), (row_done, 0), (row_done, 1), (row_done, 2), (row_done, 3),
    )
    for step, *args in steps:
        step(*args)
    for cond, d in pending:
        when(cond, d.wait_send)
    for d in (ln, lo, ls, lt):
        d.wait()
    for d in own_out:
        when(own, d.wait)


def mix_kernel(ht, sb, w, n, normed_in, mout_in, mixed, normed_out, mout_out, sem):
    i = pl.program_id(0)
    shrink = mix_share * STEP * MULT
    copies = (
        pltpu.make_async_copy(normed_in, normed_out, sem.at[0]),
        pltpu.make_async_copy(mout_in, mout_out, sem.at[1]),
    )

    @pl.when(i == 0)
    def _():
        for d in copies:
            d.start()

    g = jnp.dot(ht[0], sb[0].reshape(256, MIXCOLS), preferred_element_type=F32)
    g = g + jnp.dot(ht[1], sb[1].reshape(256, MIXCOLS), preferred_element_type=F32)
    mixed[...] = (mix_share * w[...].astype(F32) - shrink * g + (1.0 - mix_share) * n[...].astype(F32)).astype(BF16)

    @pl.when(i == pl.num_programs(0) - 1)
    def _():
        for d in copies:
            d.wait()


def local(hidden_act, residual_in, cotangent, norm_gain, inner_weight, anchor, momentum):
    hbm = pl.BlockSpec(memory_space=pl.ANY)
    away = pl.BlockSpec(memory_space=pltpu.HBM)
    vmem = pl.BlockSpec(memory_space=pltpu.VMEM)
    b16 = lambda *shape: pltpu.VMEM(shape, BF16)
    f32 = lambda *shape: pltpu.VMEM(shape, F32)
    stay = lambda v: pltpu.with_memory_space_constraint(v, pltpu.HBM)
    like = lambda *shape: jax.ShapeDtypeStruct(shape, BF16)
    normed, moment, ht, sb, nfull = pl.pallas_call(
        kernel,
        out_shape=(like(64, COLS), like(32, ROWS), like(2, ROWS, 256), like(2, 4, 64, COLS), like(ROWS, COLS)),
        in_specs=[away, away, away, vmem, away, away, away],
        out_specs=(hbm,) * 5,
        scratch_shapes=[
            b16(ROWS, COLS), b16(2, 256, ROWS), b16(2, ROWS, 256), f32(2, 4, 64, COLS), b16(2, 4, 64, COLS),
            b16(2, PIECES, 2, PIECE // 2, COLS), b16(2, PIECES, 2, PIECE, COLS), f32(PIECES, PIECE, COLS),
            b16(PIECES, PIECE, COLS), b16(PIECES, PIECE, COLS), b16(64, COLS), b16(64, COLS),
            f32(PIECES, 2, PIECE, 128), f32(PIECES, 2, PIECE, 128), b16(64, COLS), b16(64, COLS), f32(1, COLS),
            b16(ROWS, 256), b16(ROWS, 256), b16(2, ROWS, 256), b16(ROWS, 256), b16(4, 64, ROWS),
            b16(3, 64, ROWS), b16(2, 32, ROWS), b16(32, ROWS), b16(32, ROWS), b16(32, ROWS), b16(32, ROWS),
            b16(32, ROWS), b16(32, ROWS), b16(4, 2, 32, ROWS), b16(ROWS, 256),
            pltpu.SemaphoreType.DMA((NSEM,)), pltpu.SemaphoreType.DMA((NSEM,)), pltpu.SemaphoreType.DMA((24,)),
        ],
        compiler_params=pltpu.CompilerParams(
            collective_id=0, has_side_effects=True, vmem_limit_bytes=VMEM_LIMIT
        ),
    )(
        stay(hidden_act), stay(residual_in), stay(cotangent), norm_gain.reshape(16, 128), stay(inner_weight),
        stay(anchor.T), stay(momentum.T),
    )
    column = lambda i: (0, i)
    mixed, normed, moment = pl.pallas_call(
        mix_kernel,
        grid=(COLS // MIXCOLS,),
        out_shape=(like(ROWS, COLS), like(64, COLS), like(32, ROWS)),
        in_specs=[
            pl.BlockSpec((2, ROWS, 256), lambda i: (0, 0, 0)),
            pl.BlockSpec((2, 4, 64, MIXCOLS), lambda i: (0, 0, 0, i)),
            pl.BlockSpec((ROWS, MIXCOLS), column),
            pl.BlockSpec((ROWS, MIXCOLS), column),
            hbm, hbm,
        ],
        out_specs=(pl.BlockSpec((ROWS, MIXCOLS), column), hbm, hbm),
        scratch_shapes=[pltpu.SemaphoreType.DMA((2,))],
        compiler_params=pltpu.CompilerParams(vmem_limit_bytes=24 * 1024 * 1024),
    )(ht, sb, inner_weight, nfull, normed, moment)
    return (normed, mixed, moment.T)


def solution(mesh):
    in_specs = (
        P("replica", "tensor"),
        P("tensor", "replica"),
        P("tensor", "replica"),
        P(),
        P("tensor", "replica"),
        P("tensor", "replica"),
        P("tensor", "replica"),
    )
    out_specs = (P("tensor", "replica"), P("tensor", "replica"), P("tensor", "replica"))
    return jax.shard_map(local, mesh=mesh, in_specs=in_specs, out_specs=out_specs, check_vma=False)
```
